32 devices in a mesh: gx: 4 (over y, x), gy: 2 (over core), gz: 4 (over z).
Axes of the slice: x: 2, y: 2, z: 4, core: 2. Of those that a mesh axis runs over, the one named last changes fastest.
Arguments:
- trace_maps: bfloat16 [4, 2, 4, 2, 1024, 1024], P('gx', 'gy', 'gz'), may hold values from -0.109375 to 0.109375
- sources: float32 [4, 2, 4, 2, 16, 1024], P('gx', 'gy', 'gz'), may hold values from -6 to 6
- corner: int32 [1], replicated, may hold values from 0 to 7
Outputs:
- traces: bfloat16 [4, 2, 4, 2, 16, 1024], P('gx', 'gy', 'gz')
The draws below stay inside these ranges and needn't reach their ends.
All inputs are finite; a program needn't handle non-finite values.
Results may differ from the reference program's by a relative error of at most 0.012.
Values may be sent and summed in bfloat16 or wider, within the bound.
No kernel may reach another device: no remote copies, remote signals or barrier semaphores. Data moves between devices by JAX's collectives and lax.ppermute only.
A program may use at most 64 MiB of HBM per device.

```python
import jax
import jax.numpy as jnp
from jax import lax

FACE = 1024
COLS = 16
SLOTS = 2
STEPS = 6
N_GX = 4
N_GY = 2
N_GZ = 4


def levels(rng, extent, pieces, least, largest):
    level = 1.0
    for dim, shards_of in pieces:
        heights = jax.random.uniform(jax.random.fold_in(jax.random.fold_in(rng, 6), dim), (shards_of,), jnp.float32, least / len(pieces), largest / len(pieces))
        level = level * jnp.repeat(jnp.exp(heights), extent[dim] // shards_of).reshape((-1,) + (1,) * (len(extent) - 1 - dim))
    return level


def bell_draw(stream_key, shape, deviation, most, split=(), kind=jnp.bfloat16):
    values = jax.random.normal(stream_key, shape, jnp.float32) * deviation
    if len(split) > 0:
        values = levels(stream_key, shape, split, -0.22, 0.18) * values
    return jnp.clip(values, min=-most, max=most).astype(kind)


def setup_inputs(seed: int = 0) -> dict:
    splits = jax.random.split(jax.random.key(seed), 4)
    trace_maps = bell_draw(splits[0], (N_GX, N_GY, N_GZ, SLOTS, FACE, FACE), (3 * FACE) ** -0.5, 0.109375, ((0, 4), (1, 2), (2, 4)))
    sources = bell_draw(splits[1], (N_GX, N_GY, N_GZ, SLOTS, COLS, FACE), 1.0, 6.0, ((0, 4), (1, 2), (2, 4)), jnp.float32)
    corner = jax.random.randint(splits[2], (1,), 0, 8).astype(jnp.int32)
    return {"trace_maps": trace_maps, "sources": sources, "corner": corner}


def upstream(values, axis, from_lower):
    count = values.shape[axis]
    zero = jnp.zeros_like(lax.slice_in_dim(values, 0, 1, axis=axis))
    lower = jnp.concatenate([zero, lax.slice_in_dim(values, 0, count - 1, axis=axis)], axis=axis)
    upper = jnp.concatenate([lax.slice_in_dim(values, 1, count, axis=axis), zero], axis=axis)
    return jnp.where(from_lower, lower, upper)


def reference(trace_maps, sources, corner):
    code = corner[0]
    trace = sources.astype(jnp.bfloat16)
    shape = trace.shape
    flat_maps = trace_maps.reshape((-1, FACE, FACE))
    for step in range(STEPS):
        incoming = jnp.zeros(shape, jnp.float32)
        for axis in range(3):
            bit = jnp.right_shift(code, axis) & 1
            slot_bits = jnp.stack([bit, 1 - bit]).reshape((1, 1, 1, SLOTS, 1, 1))
            incoming = incoming + upstream(trace, axis, slot_bits == 1).astype(jnp.float32)
        summed = incoming.astype(jnp.bfloat16).reshape((-1, COLS, FACE))

        def apply_map(pair):
            return jnp.dot(pair[0], pair[1], preferred_element_type=jnp.float32)

        mapped = lax.map(apply_map, (summed, flat_maps)).reshape(shape)
        trace = (mapped + sources).astype(jnp.bfloat16)
    return trace
```

```python
import functools
import itertools

import jax
import jax.numpy as jnp
from jax import lax
from jax.experimental import pallas as pl
from jax.experimental.pallas import tpu as pltpu
from jax.sharding import PartitionSpec as P

STEPS = 6
AXES = ("gx", "gy", "gz")
ORDER = (0, 2, 1)
ROOM = pltpu.CompilerParams(vmem_limit_bytes=8 * 1024 * 1024)


def places(sizes):
    return itertools.product(*(range(size) for size in sizes))


def number(sizes, place):
    flat = 0
    for index, size in zip(place, sizes):
        flat = flat * size + index
    return flat


def depth_of(sizes, bits, place):
    return sum(
        index if bit else size - 1 - index for index, size, bit in zip(place, sizes, bits)
    )


def level_edges(sizes, bits, axis, level):
    edges = []
    for place in places(sizes):
        index = place[axis] + (1 if bits[axis] else -1)
        if 0 <= index < sizes[axis] and depth_of(sizes, bits, place) == level:
            edges.append((place, place[:axis] + (index,) + place[axis + 1 :]))
    return edges


def hop_edges(sizes, bits, axis, hop):
    back = tuple(1 - bit for bit in bits)
    return level_edges(sizes, bits, axis, hop - 1) + level_edges(sizes, back, axis, hop - 1)


def clash(edges):
    sources, targets = zip(*edges) if edges else ((), ())
    return len(set(sources)) < len(sources) or len(set(targets)) < len(targets)


def fits_wave(sizes):
    deepest = sum(size - 1 for size in sizes)
    return deepest <= STEPS + 1 and deepest % 2 == 1


def shared_key(axis, hop, hops):
    if axis == 1:
        return hop % 2
    if hop % 2 == 1:
        return ("odd", hop % 4)
    return ("even", 2 * hop <= hops + 1)


def pairs_of(sizes, bits, axis, hop):
    deepest = sum(size - 1 for size in sizes)
    own = hop_edges(sizes, bits, axis, hop)
    key = shared_key(axis, hop, deepest)
    edges = []
    for other in range(1, deepest + 1):
        if shared_key(axis, other, deepest) == key:
            edges += hop_edges(sizes, bits, axis, other)
    edges = sorted(set(edges))
    if clash(edges):
        edges = own
    assert not clash(edges)
    return sorted((number(sizes, source), number(sizes, target)) for source, target in edges)


def my_depth(sizes, bits):
    return depth_of(sizes, bits, tuple(lax.axis_index(axis) for axis in AXES))


def begin_kernel(sizes, bits, lead_ref, sources_ref, message_ref, traces_ref, held_ref, arrived):
    lead = lead_ref[0]
    copies = [
        pltpu.make_async_copy(
            sources_ref.at[lead if slot == 0 else 1 - lead], held_ref.at[slot], arrived.at[slot]
        )
        for slot in range(2)
    ]
    for copy in copies:
        copy.start()
    for copy in copies:
        copy.wait()
    traces_ref[...] = held_ref[...].astype(traces_ref.dtype)
    rows = held_ref.shape[1]
    if message_ref.shape[0] > rows:
        message_ref[rows:] = jnp.zeros_like(message_ref[rows:])
    entry = my_depth(sizes, bits) == 0
    message_ref[:rows] = jnp.where(entry, traces_ref[0], traces_ref[1])


def begin(sizes, bits, chains, lead, sources):
    _, rows, face = sources.shape
    vmem = pl.BlockSpec(memory_space=pltpu.VMEM)
    return pl.pallas_call(
        functools.partial(begin_kernel, sizes, bits),
        out_shape=(
            pltpu.VMEM((chains * rows, face), jnp.bfloat16),
            pltpu.VMEM(sources.shape, jnp.bfloat16),
            pltpu.VMEM(sources.shape, sources.dtype),
        ),
        in_specs=[pl.BlockSpec(memory_space=pltpu.SMEM), pl.BlockSpec(memory_space=pl.ANY)],
        out_specs=(vmem, vmem, vmem),
        scratch_shapes=[pltpu.SemaphoreType.DMA((2,))],
        compiler_params=ROOM,
        name="begin",
    )(lead, sources)


def load_kernel(lead_ref, maps_ref, after_ref, held_ref, arrived):
    lead = lead_ref[0]
    copies = [
        pltpu.make_async_copy(
            maps_ref.at[lead if slot == 0 else 1 - lead], held_ref.at[slot], arrived.at[slot]
        )
        for slot in range(2)
    ]
    for copy in copies:
        copy.start()
    for copy in copies:
        copy.wait()


def load(lead, maps, after):
    hbm = pl.BlockSpec(memory_space=pl.ANY)
    return pl.pallas_call(
        load_kernel,
        out_shape=pltpu.VMEM(maps.shape, maps.dtype),
        in_specs=[pl.BlockSpec(memory_space=pltpu.SMEM), hbm, hbm],
        out_specs=pl.BlockSpec(memory_space=pltpu.VMEM),
        scratch_shapes=[pltpu.SemaphoreType.DMA((2,))],
        compiler_params=ROOM,
        name="load",
    )(lead, maps, after)


def hop_kernel(
    hop, sizes, bits, lead_ref, x_ref, y_ref, z_ref, maps_ref, sources_ref, old_ref, *results
):
    deepest = sum(size - 1 for size in sizes)
    depth = my_depth(sizes, bits)
    back = deepest - depth
    last = hop == deepest
    traces_ref = results[-1]
    rows = sources_ref.shape[1]

    def place_of(slot):
        return jnp.where(lead_ref[0] == 0, slot, 1 - slot) if last else slot

    for slot in range(2):
        traces_ref[place_of(slot)] = old_ref[slot]

    @pl.when((depth == hop) | (back == hop))
    def _():
        slot = jnp.where(depth == hop, 0, 1)
        summed = x_ref[...].astype(jnp.float32) + y_ref[...].astype(jnp.float32)
        summed = summed + z_ref[...].astype(jnp.float32)
        mapped = jnp.dot(
            summed.astype(jnp.bfloat16), maps_ref[slot], preferred_element_type=jnp.float32
        )
        source = sources_ref[slot]
        for chain in range(mapped.shape[0] // rows):
            part = slice(chain * rows, (chain + 1) * rows)
            new = (mapped[part] + source).astype(jnp.bfloat16)
            if not last:
                results[0][part] = new
            if chain == max(0, hop - STEPS):
                traces_ref[place_of(slot)] = new


def take_hop(hop, sizes, bits, lead, came, maps, sources, traces):
    last = hop == sum(size - 1 for size in sizes)
    vmem = pl.BlockSpec(memory_space=pltpu.VMEM)
    held = [pltpu.with_memory_space_constraint(a, pltpu.VMEM) for a in came]
    held += [pltpu.with_memory_space_constraint(a, pltpu.VMEM) for a in (maps, sources, traces)]
    shapes = (jax.ShapeDtypeStruct(traces.shape, traces.dtype),)
    if not last:
        shapes = (
            pltpu.VMEM(came[0].shape, came[0].dtype),
            pltpu.VMEM(traces.shape, traces.dtype),
        )
    results = pl.pallas_call(
        functools.partial(hop_kernel, hop, sizes, bits),
        out_shape=shapes,
        in_specs=[pl.BlockSpec(memory_space=pltpu.SMEM if last else pl.ANY)] + [vmem] * 6,
        out_specs=(vmem,) * len(shapes),
        compiler_params=ROOM,
        name=f"hop{hop}",
    )(lead, *held)
    return results[0], results[-1]


def wave(sizes, bits, lead, maps, sources):
    deepest = sum(size - 1 for size in sizes)
    chains = max(0, deepest - STEPS) + 1
    message, traces, sources = begin(sizes, bits, chains, lead, sources)
    for hop in range(1, deepest + 1):
        came = [None] * 3
        for axis in ORDER:
            came[axis] = lax.ppermute(message, AXES, pairs_of(sizes, bits, axis, hop))
        if hop == 1:
            maps = load(lead, maps, message)
        message, traces = take_hop(hop, sizes, bits, lead, came, maps, sources, traces)
    return traces


def passed_along(array, axis, by):
    devices = lax.axis_size(axis)
    pairs = [(i, i + by) for i in range(devices) if 0 <= i + by < devices]
    return lax.ppermute(array, axis, pairs)


def stepped(code, maps, sources):
    traces = sources.astype(jnp.bfloat16)
    for _ in range(STEPS):
        incoming = jnp.zeros(sources.shape, jnp.float32)
        for position, axis in enumerate(AXES):
            up = (jnp.right_shift(code, position) & 1) == 1
            lower = passed_along(jnp.where(up, traces[0], traces[1]), axis, 1)
            upper = passed_along(jnp.where(up, traces[1], traces[0]), axis, -1)
            came = jnp.stack([jnp.where(up, lower, upper), jnp.where(up, upper, lower)])
            incoming = incoming + came.astype(jnp.float32)
        mapped = jnp.einsum(
            "scf,sfg->scg", incoming.astype(jnp.bfloat16), maps, preferred_element_type=jnp.float32
        )
        traces = (mapped + sources).astype(jnp.bfloat16)
    return traces


def solution(mesh):
    sizes = tuple(mesh.shape[axis] for axis in AXES)

    def shards(trace_maps, sources, corner):
        maps = trace_maps[0, 0, 0]
        rows = sources[0, 0, 0]
        code = corner[0]
        if not fits_wave(sizes):
            return stepped(code, maps, rows)[None, None, None]
        lead = 1 - (jnp.right_shift(code, 1) & 1)
        code = jnp.where(lead == 1, 7 - code, code)
        kind = (code & 1) + 2 * (jnp.right_shift(code, 2) & 1)

        def branch(kind):
            bits = (kind & 1, 1, kind >> 1)
            return lambda *operands: wave(sizes, bits, *operands)

        traces = lax.switch(
            kind, [branch(kind) for kind in range(4)], lead.reshape(1), maps, rows
        )
        return traces[None, None, None]

    return jax.shard_map(
        shards,
        mesh=mesh,
        in_specs=(
            P("gx", "gy", "gz", None, None, None),
            P("gx", "gy", "gz", None, None, None),
            P(),
        ),
        out_specs=P("gx", "gy", "gz", None, None, None),
        check_vma=False,
    )
```

```python
import functools
import itertools

import jax
import jax.numpy as jnp
from jax import lax
from jax.experimental import pallas as pl
from jax.experimental.pallas import tpu as pltpu
from jax.sharding import PartitionSpec as P

STEPS = 6
AXES = ("gx", "gy", "gz")
ORDER = (0, 2, 1)
ROOM = pltpu.CompilerParams(vmem_limit_bytes=8 * 1024 * 1024)


def places(sizes):
    return itertools.product(*(range(size) for size in sizes))


def number(sizes, place):
    flat = 0
    for index, size in zip(place, sizes):
        flat = flat * size + index
    return flat


def depth_of(sizes, bits, place):
    return sum(
        index if bit else size - 1 - index for index, size, bit in zip(place, sizes, bits)
    )


def level_edges(sizes, bits, axis, level):
    edges = []
    for place in places(sizes):
        index = place[axis] + (1 if bits[axis] else -1)
        if 0 <= index < sizes[axis] and depth_of(sizes, bits, place) == level:
            edges.append((place, place[:axis] + (index,) + place[axis + 1 :]))
    return edges


def hop_edges(sizes, bits, axis, hop):
    back = tuple(1 - bit for bit in bits)
    return level_edges(sizes, bits, axis, hop - 1) + level_edges(sizes, back, axis, hop - 1)


def clash(edges):
    sources, targets = zip(*edges) if edges else ((), ())
    return len(set(sources)) < len(sources) or len(set(targets)) < len(targets)


def fits_wave(sizes):
    deepest = sum(size - 1 for size in sizes)
    return deepest <= STEPS + 1 and deepest % 2 == 1


SHARED = (
    ((1, 2), (3, 7), (4, 6), (5,)),
    ((1, 7), (2, 6), (3, 5), (4,)),
    ((1, 2, 4), (3, 7), (5, 6)),
)


def pairs_of(sizes, bits, axis, hop):
    deepest = sum(size - 1 for size in sizes)
    own = hop_edges(sizes, bits, axis, hop)
    group = next((group for group in SHARED[axis] if hop in group), (hop,))
    edges = [edge for other in group if other <= deepest for edge in hop_edges(sizes, bits, axis, other)]
    edges = sorted(set(edges))
    if clash(edges):
        edges = own
    assert not clash(edges)
    return sorted((number(sizes, source), number(sizes, target)) for source, target in edges)


def my_depth(sizes, bits):
    return depth_of(sizes, bits, tuple(lax.axis_index(axis) for axis in AXES))


def begin_kernel(sizes, bits, lead_ref, sources_ref, message_ref, traces_ref, held_ref, arrived):
    lead = lead_ref[0]
    copies = [
        pltpu.make_async_copy(
            sources_ref.at[lead if slot == 0 else 1 - lead], held_ref.at[slot], arrived.at[slot]
        )
        for slot in range(2)
    ]
    for copy in copies:
        copy.start()
    for copy in copies:
        copy.wait()
    traces_ref[...] = held_ref[...].astype(traces_ref.dtype)
    rows = held_ref.shape[1]
    if message_ref.shape[0] > rows:
        message_ref[rows:] = jnp.zeros_like(message_ref[rows:])
    entry = my_depth(sizes, bits) == 0
    message_ref[:rows] = jnp.where(entry, traces_ref[0], traces_ref[1])


def begin(sizes, bits, chains, lead, sources):
    _, rows, face = sources.shape
    vmem = pl.BlockSpec(memory_space=pltpu.VMEM)
    return pl.pallas_call(
        functools.partial(begin_kernel, sizes, bits),
        out_shape=(
            pltpu.VMEM((chains * rows, face), jnp.bfloat16),
            pltpu.VMEM(sources.shape, jnp.bfloat16),
            pltpu.VMEM(sources.shape, sources.dtype),
        ),
        in_specs=[pl.BlockSpec(memory_space=pltpu.SMEM), pl.BlockSpec(memory_space=pl.ANY)],
        out_specs=(vmem, vmem, vmem),
        scratch_shapes=[pltpu.SemaphoreType.DMA((2,))],
        compiler_params=ROOM,
        name="begin",
    )(lead, sources)


def load_kernel(lead_ref, maps_ref, after_ref, held_ref, arrived):
    lead = lead_ref[0]
    copies = [
        pltpu.make_async_copy(
            maps_ref.at[lead if slot == 0 else 1 - lead], held_ref.at[slot], arrived.at[slot]
        )
        for slot in range(2)
    ]
    for copy in copies:
        copy.start()
    for copy in copies:
        copy.wait()


def load(lead, maps, after):
    hbm = pl.BlockSpec(memory_space=pl.ANY)
    return pl.pallas_call(
        load_kernel,
        out_shape=pltpu.VMEM(maps.shape, maps.dtype),
        in_specs=[pl.BlockSpec(memory_space=pltpu.SMEM), hbm, hbm],
        out_specs=pl.BlockSpec(memory_space=pltpu.VMEM),
        scratch_shapes=[pltpu.SemaphoreType.DMA((2,))],
        compiler_params=ROOM,
        name="load",
    )(lead, maps, after)


def hop_kernel(
    hop, sizes, bits, lead_ref, y_ref, z_ref, x_ref, maps_ref, sources_ref, old_ref, *results
):
    deepest = sum(size - 1 for size in sizes)
    depth = my_depth(sizes, bits)
    back = deepest - depth
    last = hop == deepest
    traces_ref = results[-1]
    rows = sources_ref.shape[1]

    def place_of(slot):
        return jnp.where(lead_ref[0] == 0, slot, 1 - slot) if last else slot

    for slot in range(2):
        traces_ref[place_of(slot)] = old_ref[slot]

    @pl.when((depth == hop) | (back == hop))
    def _():
        slot = jnp.where(depth == hop, 0, 1)
        summed = x_ref[...].astype(jnp.float32) + y_ref[...].astype(jnp.float32)
        summed = summed + z_ref[...].astype(jnp.float32)
        mapped = jnp.dot(
            summed.astype(jnp.bfloat16), maps_ref[slot], preferred_element_type=jnp.float32
        )
        source = sources_ref[slot]
        for chain in range(mapped.shape[0] // rows):
            part = slice(chain * rows, (chain + 1) * rows)
            new = (mapped[part] + source).astype(jnp.bfloat16)
            if not last:
                results[0][part] = new
            if chain == max(0, hop - STEPS):
                traces_ref[place_of(slot)] = new


def take_hop(hop, sizes, bits, lead, came, maps, sources, traces):
    last = hop == sum(size - 1 for size in sizes)
    vmem = pl.BlockSpec(memory_space=pltpu.VMEM)
    came = [came[axis] for axis in reversed(ORDER)]
    held = [pltpu.with_memory_space_constraint(a, pltpu.VMEM) for a in came]
    held += [pltpu.with_memory_space_constraint(a, pltpu.VMEM) for a in (maps, sources, traces)]
    shapes = (jax.ShapeDtypeStruct(traces.shape, traces.dtype),)
    if not last:
        shapes = (
            pltpu.VMEM(came[0].shape, came[0].dtype),
            pltpu.VMEM(traces.shape, traces.dtype),
        )
    results = pl.pallas_call(
        functools.partial(hop_kernel, hop, sizes, bits),
        out_shape=shapes,
        in_specs=[pl.BlockSpec(memory_space=pltpu.SMEM if last else pl.ANY)] + [vmem] * 6,
        out_specs=(vmem,) * len(shapes),
        compiler_params=ROOM,
        name=f"hop{hop}",
    )(lead, *held)
    return results[0], results[-1]


def wave(sizes, bits, lead, maps, sources):
    deepest = sum(size - 1 for size in sizes)
    chains = max(0, deepest - STEPS) + 1
    message, traces, sources = begin(sizes, bits, chains, lead, sources)
    for hop in range(1, deepest + 1):
        came = [None] * 3
        for axis in ORDER:
            came[axis] = lax.ppermute(message, AXES, pairs_of(sizes, bits, axis, hop))
        if hop == 1:
            maps = load(lead, maps, message)
        message, traces = take_hop(hop, sizes, bits, lead, came, maps, sources, traces)
    return traces


def passed_along(array, axis, by):
    devices = lax.axis_size(axis)
    pairs = [(i, i + by) for i in range(devices) if 0 <= i + by < devices]
    return lax.ppermute(array, axis, pairs)


def stepped(code, maps, sources):
    traces = sources.astype(jnp.bfloat16)
    for _ in range(STEPS):
        incoming = jnp.zeros(sources.shape, jnp.float32)
        for position, axis in enumerate(AXES):
            up = (jnp.right_shift(code, position) & 1) == 1
            lower = passed_along(jnp.where(up, traces[0], traces[1]), axis, 1)
            upper = passed_along(jnp.where(up, traces[1], traces[0]), axis, -1)
            came = jnp.stack([jnp.where(up, lower, upper), jnp.where(up, upper, lower)])
            incoming = incoming + came.astype(jnp.float32)
        mapped = jnp.einsum(
            "scf,sfg->scg", incoming.astype(jnp.bfloat16), maps, preferred_element_type=jnp.float32
        )
        traces = (mapped + sources).astype(jnp.bfloat16)
    return traces


def solution(mesh):
    sizes = tuple(mesh.shape[axis] for axis in AXES)

    def shards(trace_maps, sources, corner):
        maps = trace_maps[0, 0, 0]
        rows = sources[0, 0, 0]
        code = corner[0]
        if not fits_wave(sizes):
            return stepped(code, maps, rows)[None, None, None]
        lead = 1 - (jnp.right_shift(code, 1) & 1)
        code = jnp.where(lead == 1, 7 - code, code)
        kind = (code & 1) + 2 * (jnp.right_shift(code, 2) & 1)

        def branch(kind):
            bits = (kind & 1, 1, kind >> 1)
            return lambda *operands: wave(sizes, bits, *operands)

        traces = lax.switch(
            kind, [branch(kind) for kind in range(4)], lead.reshape(1), maps, rows
        )
        return traces[None, None, None]

    return jax.shard_map(
        shards,
        mesh=mesh,
        in_specs=(
            P("gx", "gy", "gz", None, None, None),
            P("gx", "gy", "gz", None, None, None),
            P(),
        ),
        out_specs=P("gx", "gy", "gz", None, None, None),
        check_vma=False,
    )
```

```python
import functools
import itertools

import jax
import jax.numpy as jnp
from jax import lax
from jax.experimental import pallas as pl
from jax.experimental.pallas import tpu as pltpu
from jax.sharding import PartitionSpec as P

STEPS = 6
AXES = ("gx", "gy", "gz")
ORDER = (0, 2, 1)
ROOM = pltpu.CompilerParams(vmem_limit_bytes=8 * 1024 * 1024)


def places(sizes):
    return itertools.product(*(range(size) for size in sizes))


def number(sizes, place):
    flat = 0
    for index, size in zip(place, sizes):
        flat = flat * size + index
    return flat


def depth_of(sizes, bits, place):
    return sum(
        index if bit else size - 1 - index for index, size, bit in zip(place, sizes, bits)
    )


def level_edges(sizes, bits, axis, level):
    edges = []
    for place in places(sizes):
        index = place[axis] + (1 if bits[axis] else -1)
        if 0 <= index < sizes[axis] and depth_of(sizes, bits, place) == level:
            edges.append((place, place[:axis] + (index,) + place[axis + 1 :]))
    return edges


def hop_edges(sizes, bits, axis, hop):
    back = tuple(1 - bit for bit in bits)
    return level_edges(sizes, bits, axis, hop - 1) + level_edges(sizes, back, axis, hop - 1)


def clash(edges):
    sources, targets = zip(*edges) if edges else ((), ())
    return len(set(sources)) < len(sources) or len(set(targets)) < len(targets)


def fits_wave(sizes):
    deepest = sum(size - 1 for size in sizes)
    return deepest <= STEPS + 1 and deepest % 2 == 1


SHARED = (
    (
        (0, 1, 2, 3, 4, 5, 6),
        (7, 8, 9, 3, 10, 11, 6),
        (7, 9, 8, 12, 11, 10, 6),
        (0, 2, 1, 12, 5, 4, 6),
    ),
    (
        (0, 1, 2, 3, 1, 4, 5),
        (0, 2, 4, 6, 7, 2, 5),
        (5, 2, 8, 9, 4, 2, 3),
        (5, 4, 1, 3, 2, 1, 0),
    ),
    (
        (0, 1, 2, 3, 4, 5, 6),
        (7, 8, 9, 10, 11, 12, 6),
        (8, 7, 13, 3, 12, 11, 6),
        (1, 0, 14, 10, 5, 4, 6),
    ),
)


def kind_bits(kind):
    return (kind & 1, 1, kind >> 1)


def pairs_of(sizes, bits, axis, hop):
    deepest = sum(size - 1 for size in sizes)
    own = hop_edges(sizes, bits, axis, hop)
    number_of = SHARED[axis][bits[0] + 2 * bits[2]][hop - 1]
    edges = set(own)
    for kind, row in enumerate(SHARED[axis]):
        for other, found in enumerate(row, 1):
            if found == number_of and other <= deepest:
                edges.update(hop_edges(sizes, kind_bits(kind), axis, other))
    if clash(sorted(edges)):
        edges = set(own)
    assert not clash(sorted(edges))
    return sorted((number(sizes, source), number(sizes, target)) for source, target in edges)


def my_depth(sizes, bits):
    return depth_of(sizes, bits, tuple(lax.axis_index(axis) for axis in AXES))


def chains_sent(hop, deepest):
    return range(max(0, hop - STEPS), min(max(0, deepest - STEPS), hop - 1) + 1)


def begin_kernel(sizes, bits, lead_hbm, sources_hbm, message_ref, traces_ref, held_ref, lead_ref, raw_ref, arrived):
    copies = [
        pltpu.make_async_copy(sources_hbm, raw_ref, arrived.at[0]),
        pltpu.make_async_copy(lead_hbm, lead_ref, arrived.at[1]),
    ]
    for copy in copies:
        copy.start()
    for copy in copies:
        copy.wait()
    lead = lead_ref[0]
    entry = my_depth(sizes, bits) == 0
    message_ref[...] = raw_ref[jnp.where(entry, lead, 1 - lead)].astype(message_ref.dtype)
    for slot in range(2):
        source = raw_ref[lead if slot == 0 else 1 - lead]
        held_ref[slot] = source
        traces_ref[slot] = source.astype(traces_ref.dtype)


def begin(sizes, bits, lead, sources):
    vmem = pl.BlockSpec(memory_space=pltpu.VMEM)
    hbm = pl.BlockSpec(memory_space=pl.ANY)
    return pl.pallas_call(
        functools.partial(begin_kernel, sizes, bits),
        out_shape=(
            pltpu.VMEM(sources.shape[1:], jnp.bfloat16),
            pltpu.VMEM(sources.shape, jnp.bfloat16),
            pltpu.VMEM(sources.shape, sources.dtype),
        ),
        in_specs=[hbm, hbm],
        out_specs=(vmem, vmem, vmem),
        scratch_shapes=[
            pltpu.SMEM(lead.shape, lead.dtype),
            pltpu.VMEM(sources.shape, sources.dtype),
            pltpu.SemaphoreType.DMA((2,)),
        ],
        compiler_params=ROOM,
        name="begin",
    )(lead, sources)


def load_kernel(lead_ref, maps_ref, after_ref, held_ref, arrived):
    lead = lead_ref[0]
    copies = [
        pltpu.make_async_copy(
            maps_ref.at[lead if slot == 0 else 1 - lead], held_ref.at[slot], arrived.at[slot]
        )
        for slot in range(2)
    ]
    for copy in copies:
        copy.start()
    for copy in copies:
        copy.wait()


def load(lead, maps, after):
    hbm = pl.BlockSpec(memory_space=pl.ANY)
    return pl.pallas_call(
        load_kernel,
        out_shape=pltpu.VMEM(maps.shape, maps.dtype),
        in_specs=[pl.BlockSpec(memory_space=pltpu.SMEM), hbm, hbm],
        out_specs=pl.BlockSpec(memory_space=pltpu.VMEM),
        scratch_shapes=[pltpu.SemaphoreType.DMA((2,))],
        compiler_params=ROOM,
        name="load",
    )(lead, maps, after)


def hop_kernel(
    hop, sizes, bits, lead_ref, y_ref, z_ref, x_ref, maps_ref, sources_ref, old_ref, *results
):
    deepest = sum(size - 1 for size in sizes)
    depth = my_depth(sizes, bits)
    back = deepest - depth
    last = hop == deepest
    traces_ref = results[-1]
    rows = sources_ref.shape[1]

    def place_of(slot):
        return jnp.where(lead_ref[0] == 0, slot, 1 - slot) if last else slot

    for slot in range(2):
        traces_ref[place_of(slot)] = old_ref[slot]

    @pl.when((depth == hop) | (back == hop))
    def _():
        slot = jnp.where(depth == hop, 0, 1)
        summed = None
        for axis, ref in enumerate((x_ref, y_ref, z_ref)):
            index = lax.axis_index(AXES[axis])
            lower, upper = index > 0, index < sizes[axis] - 1
            inside = jnp.where(
                (depth == hop) == bool(bits[axis]), lower.astype(jnp.int32), upper.astype(jnp.int32)
            )
            came = jnp.where(inside == 1, ref[...].astype(jnp.float32), 0.0)
            summed = came if summed is None else summed + came
        mapped = jnp.dot(
            summed.astype(jnp.bfloat16), maps_ref[slot], preferred_element_type=jnp.float32
        )
        source = sources_ref[slot]
        came = chains_sent(hop, deepest)
        kept = came if last else chains_sent(hop + 1, deepest)
        for chain in sorted({*came, *kept}):
            if chain in came:
                at = came.index(chain) * rows
                new = (mapped[at : at + rows] + source).astype(jnp.bfloat16)
            else:
                new = source.astype(jnp.bfloat16)
            if not last and chain in kept:
                at = kept.index(chain) * rows
                results[0][at : at + rows] = new
            if chain == max(0, hop - STEPS):
                traces_ref[place_of(slot)] = new


def take_hop(hop, sizes, bits, lead, came, maps, sources, traces):
    deepest = sum(size - 1 for size in sizes)
    last = hop == deepest
    vmem = pl.BlockSpec(memory_space=pltpu.VMEM)
    came = [came[axis] for axis in reversed(ORDER)]
    held = [pltpu.with_memory_space_constraint(a, pltpu.VMEM) for a in came]
    held += [pltpu.with_memory_space_constraint(a, pltpu.VMEM) for a in (maps, sources, traces)]
    shapes = (jax.ShapeDtypeStruct(traces.shape, traces.dtype),)
    if not last:
        shapes = (
            pltpu.VMEM(
                (len(chains_sent(hop + 1, deepest)) * sources.shape[1], sources.shape[2]), traces.dtype
            ),
            pltpu.VMEM(traces.shape, traces.dtype),
        )
    results = pl.pallas_call(
        functools.partial(hop_kernel, hop, sizes, bits),
        out_shape=shapes,
        in_specs=[pl.BlockSpec(memory_space=pltpu.SMEM if last else pl.ANY)] + [vmem] * 6,
        out_specs=(vmem,) * len(shapes),
        compiler_params=ROOM,
        name=f"hop{hop}",
    )(lead, *held)
    return results[0], results[-1]


def wave(sizes, bits, lead, maps, sources):
    deepest = sum(size - 1 for size in sizes)
    message, traces, sources = begin(sizes, bits, lead, sources)
    for hop in range(1, deepest + 1):
        came = [None] * 3
        for axis in ORDER:
            came[axis] = lax.ppermute(message, AXES, pairs_of(sizes, bits, axis, hop))
        if hop == 1:
            maps = load(lead, maps, message)
        message, traces = take_hop(hop, sizes, bits, lead, came, maps, sources, traces)
    return traces


def passed_along(array, axis, by):
    devices = lax.axis_size(axis)
    pairs = [(i, i + by) for i in range(devices) if 0 <= i + by < devices]
    return lax.ppermute(array, axis, pairs)


def stepped(code, maps, sources):
    traces = sources.astype(jnp.bfloat16)
    for _ in range(STEPS):
        incoming = jnp.zeros(sources.shape, jnp.float32)
        for position, axis in enumerate(AXES):
            up = (jnp.right_shift(code, position) & 1) == 1
            lower = passed_along(jnp.where(up, traces[0], traces[1]), axis, 1)
            upper = passed_along(jnp.where(up, traces[1], traces[0]), axis, -1)
            came = jnp.stack([jnp.where(up, lower, upper), jnp.where(up, upper, lower)])
            incoming = incoming + came.astype(jnp.float32)
        mapped = jnp.einsum(
            "scf,sfg->scg", incoming.astype(jnp.bfloat16), maps, preferred_element_type=jnp.float32
        )
        traces = (mapped + sources).astype(jnp.bfloat16)
    return traces


def solution(mesh):
    sizes = tuple(mesh.shape[axis] for axis in AXES)

    def shards(trace_maps, sources, corner):
        maps = trace_maps[0, 0, 0]
        rows = sources[0, 0, 0]
        code = corner[0]
        if not fits_wave(sizes):
            return stepped(code, maps, rows)[None, None, None]
        lead = 1 - (jnp.right_shift(code, 1) & 1)
        code = jnp.where(lead == 1, 7 - code, code)
        kind = (code & 1) + 2 * (jnp.right_shift(code, 2) & 1)

        def branch(kind):
            return lambda *operands: wave(sizes, kind_bits(kind), *operands)

        traces = lax.switch(
            kind, [branch(kind) for kind in range(4)], lead.reshape(1), maps, rows
        )
        return traces[None, None, None]

    return jax.shard_map(
        shards,
        mesh=mesh,
        in_specs=(
            P("gx", "gy", "gz", None, None, None),
            P("gx", "gy", "gz", None, None, None),
            P(),
        ),
        out_specs=P("gx", "gy", "gz", None, None, None),
        check_vma=False,
    )
```

```python
import functools
import itertools

import jax
import jax.numpy as jnp
from jax import lax
from jax.experimental import pallas as pl
from jax.experimental.pallas import tpu as pltpu
from jax.sharding import PartitionSpec as P

STEPS = 6
AXES = ("gx", "gy", "gz")
ORDER = (0, 2, 1)
ROOM = pltpu.CompilerParams(vmem_limit_bytes=8 * 1024 * 1024)


def places(sizes):
    return itertools.product(*(range(size) for size in sizes))


def number(sizes, place):
    flat = 0
    for index, size in zip(place, sizes):
        flat = flat * size + index
    return flat


def depth_of(sizes, bits, place):
    return sum(
        index if bit else size - 1 - index for index, size, bit in zip(place, sizes, bits)
    )


def level_edges(sizes, bits, axis, level):
    edges = []
    for place in places(sizes):
        index = place[axis] + (1 if bits[axis] else -1)
        if 0 <= index < sizes[axis] and depth_of(sizes, bits, place) == level:
            edges.append((place, place[:axis] + (index,) + place[axis + 1 :]))
    return edges


def hop_edges(sizes, bits, axis, hop):
    back = tuple(1 - bit for bit in bits)
    return level_edges(sizes, bits, axis, hop - 1) + level_edges(sizes, back, axis, hop - 1)


def clash(edges):
    sources, targets = zip(*edges) if edges else ((), ())
    return len(set(sources)) < len(sources) or len(set(targets)) < len(targets)


def fits_wave(sizes):
    deepest = sum(size - 1 for size in sizes)
    return deepest <= STEPS + 1 and deepest % 2 == 1


SHARED = (
    (
        (0, 1, 2, -1, 3, 4, 3),
        (0, 5, 6, -2, 7, 8, 9),
        (9, 6, 5, -3, 8, 7, 8),
        (1, 2, 10, -4, 4, 3, 4),
    ),
    (
        (0, 1, 2, 3, 0, 4, 5),
        (6, 7, 8, 9, 6, 5, 4),
        (7, 5, 6, 10, 11, 7, 1),
        (2, 4, 0, 12, 2, 1, 4),
    ),
    (
        (0, 1, 2, -1, 3, 4, 5),
        (6, 7, 8, -2, 9, 10, 9),
        (5, 6, 7, -3, 10, 9, 10),
        (5, 0, 1, -4, 4, 3, 4),
    ),
)


def kind_bits(kind):
    return (kind & 1, 1, kind >> 1)


def swaps_of(sizes, axis, edges):
    twins = dict(edges)
    twins.update((target, source) for source, target in edges)
    for place in places(sizes):
        if place not in twins:
            line = [place[:axis] + (i,) + place[axis + 1 :] for i in range(sizes[axis])]
            left = [other for other in line if other not in twins and other != place]
            if left:
                twins[place], twins[left[0]] = left[0], place
    return set(twins.items())


def pairs_of(sizes, bits, axis, hop):
    deepest = sum(size - 1 for size in sizes)
    own = set(hop_edges(sizes, bits, axis, hop))
    number_of = SHARED[axis][bits[0] + 2 * bits[2]][hop - 1]
    edges = set(own)
    for kind, row in enumerate(SHARED[axis]):
        for other, found in enumerate(row, 1):
            if found == number_of and other <= deepest:
                edges.update(hop_edges(sizes, kind_bits(kind), axis, other))
    if number_of < 0:
        edges = swaps_of(sizes, axis, edges)
    if clash(sorted(edges)):
        edges = own
    assert not clash(sorted(edges)) and own <= edges
    return sorted((number(sizes, source), number(sizes, target)) for source, target in edges)


def my_depth(sizes, bits):
    return depth_of(sizes, bits, tuple(lax.axis_index(axis) for axis in AXES))


def chains_sent(hop, deepest):
    return range(max(0, hop - STEPS), min(max(0, deepest - STEPS), hop - 1) + 1)


def begin_kernel(sizes, bits, lead_hbm, sources_hbm, message_ref, traces_ref, held_ref, lead_ref, raw_ref, arrived):
    copies = [
        pltpu.make_async_copy(sources_hbm, raw_ref, arrived.at[0]),
        pltpu.make_async_copy(lead_hbm, lead_ref, arrived.at[1]),
    ]
    for copy in copies:
        copy.start()
    for copy in copies:
        copy.wait()
    lead = lead_ref[0]
    entry = my_depth(sizes, bits) == 0
    message_ref[...] = raw_ref[jnp.where(entry, lead, 1 - lead)].astype(message_ref.dtype)
    for slot in range(2):
        source = raw_ref[lead if slot == 0 else 1 - lead]
        held_ref[slot] = source
        traces_ref[slot] = source.astype(traces_ref.dtype)


def begin(sizes, bits, lead, sources):
    vmem = pl.BlockSpec(memory_space=pltpu.VMEM)
    hbm = pl.BlockSpec(memory_space=pl.ANY)
    return pl.pallas_call(
        functools.partial(begin_kernel, sizes, bits),
        out_shape=(
            pltpu.VMEM(sources.shape[1:], jnp.bfloat16),
            pltpu.VMEM(sources.shape, jnp.bfloat16),
            pltpu.VMEM(sources.shape, sources.dtype),
        ),
        in_specs=[hbm, hbm],
        out_specs=(vmem, vmem, vmem),
        scratch_shapes=[
            pltpu.SMEM(lead.shape, lead.dtype),
            pltpu.VMEM(sources.shape, sources.dtype),
            pltpu.SemaphoreType.DMA((2,)),
        ],
        compiler_params=ROOM,
        name="begin",
    )(lead, sources)


def load_kernel(lead_ref, maps_ref, after_ref, held_ref, arrived):
    lead = lead_ref[0]
    copies = [
        pltpu.make_async_copy(
            maps_ref.at[lead if slot == 0 else 1 - lead], held_ref.at[slot], arrived.at[slot]
        )
        for slot in range(2)
    ]
    for copy in copies:
        copy.start()
    for copy in copies:
        copy.wait()


def load(lead, maps, after):
    hbm = pl.BlockSpec(memory_space=pl.ANY)
    return pl.pallas_call(
        load_kernel,
        out_shape=pltpu.VMEM(maps.shape, maps.dtype),
        in_specs=[pl.BlockSpec(memory_space=pltpu.SMEM), hbm, hbm],
        out_specs=pl.BlockSpec(memory_space=pltpu.VMEM),
        scratch_shapes=[pltpu.SemaphoreType.DMA((2,))],
        compiler_params=ROOM,
        name="load",
    )(lead, maps, after)


def hop_kernel(
    hop, sizes, bits, lead_ref, y_ref, z_ref, x_ref, maps_ref, sources_ref, old_ref, *results
):
    deepest = sum(size - 1 for size in sizes)
    depth = my_depth(sizes, bits)
    back = deepest - depth
    last = hop == deepest
    traces_ref = results[-1]
    rows = sources_ref.shape[1]

    def place_of(slot):
        return jnp.where(lead_ref[0] == 0, slot, 1 - slot) if last else slot

    for slot in range(2):
        traces_ref[place_of(slot)] = old_ref[slot]

    @pl.when((depth == hop) | (back == hop))
    def _():
        slot = jnp.where(depth == hop, 0, 1)
        summed = None
        for axis, ref in enumerate((x_ref, y_ref, z_ref)):
            index = lax.axis_index(AXES[axis])
            lower, upper = index > 0, index < sizes[axis] - 1
            inside = jnp.where(
                (depth == hop) == bool(bits[axis]), lower.astype(jnp.int32), upper.astype(jnp.int32)
            )
            came = jnp.where(inside == 1, ref[...].astype(jnp.float32), 0.0)
            summed = came if summed is None else summed + came
        mapped = jnp.dot(
            summed.astype(jnp.bfloat16), maps_ref[slot], preferred_element_type=jnp.float32
        )
        source = sources_ref[slot]
        came = chains_sent(hop, deepest)
        kept = came if last else chains_sent(hop + 1, deepest)
        for chain in sorted({*came, *kept}):
            if chain in came:
                at = came.index(chain) * rows
                new = (mapped[at : at + rows] + source).astype(jnp.bfloat16)
            else:
                new = source.astype(jnp.bfloat16)
            if not last and chain in kept:
                at = kept.index(chain) * rows
                results[0][at : at + rows] = new
            if chain == max(0, hop - STEPS):
                traces_ref[place_of(slot)] = new


def take_hop(hop, sizes, bits, lead, came, maps, sources, traces):
    deepest = sum(size - 1 for size in sizes)
    last = hop == deepest
    vmem = pl.BlockSpec(memory_space=pltpu.VMEM)
    came = [came[axis] for axis in reversed(ORDER)]
    held = [pltpu.with_memory_space_constraint(a, pltpu.VMEM) for a in came]
    held += [pltpu.with_memory_space_constraint(a, pltpu.VMEM) for a in (maps, sources, traces)]
    shapes = (jax.ShapeDtypeStruct(traces.shape, traces.dtype),)
    if not last:
        shapes = (
            pltpu.VMEM(
                (len(chains_sent(hop + 1, deepest)) * sources.shape[1], sources.shape[2]), traces.dtype
            ),
            pltpu.VMEM(traces.shape, traces.dtype),
        )
    results = pl.pallas_call(
        functools.partial(hop_kernel, hop, sizes, bits),
        out_shape=shapes,
        in_specs=[pl.BlockSpec(memory_space=pltpu.SMEM if last else pl.ANY)] + [vmem] * 6,
        out_specs=(vmem,) * len(shapes),
        compiler_params=ROOM,
        name=f"hop{hop}",
    )(lead, *held)
    return results[0], results[-1]


def wave(sizes, bits, lead, maps, sources):
    deepest = sum(size - 1 for size in sizes)
    message, traces, sources = begin(sizes, bits, lead, sources)
    for hop in range(1, deepest + 1):
        came = [None] * 3
        for axis in ORDER:
            came[axis] = lax.ppermute(message, AXES, pairs_of(sizes, bits, axis, hop))
        if hop == 1:
            maps = load(lead, maps, message)
        message, traces = take_hop(hop, sizes, bits, lead, came, maps, sources, traces)
    return traces


def passed_along(array, axis, by):
    devices = lax.axis_size(axis)
    pairs = [(i, i + by) for i in range(devices) if 0 <= i + by < devices]
    return lax.ppermute(array, axis, pairs)


def stepped(code, maps, sources):
    traces = sources.astype(jnp.bfloat16)
    for _ in range(STEPS):
        incoming = jnp.zeros(sources.shape, jnp.float32)
        for position, axis in enumerate(AXES):
            up = (jnp.right_shift(code, position) & 1) == 1
            lower = passed_along(jnp.where(up, traces[0], traces[1]), axis, 1)
            upper = passed_along(jnp.where(up, traces[1], traces[0]), axis, -1)
            came = jnp.stack([jnp.where(up, lower, upper), jnp.where(up, upper, lower)])
            incoming = incoming + came.astype(jnp.float32)
        mapped = jnp.einsum(
            "scf,sfg->scg", incoming.astype(jnp.bfloat16), maps, preferred_element_type=jnp.float32
        )
        traces = (mapped + sources).astype(jnp.bfloat16)
    return traces


def solution(mesh):
    sizes = tuple(mesh.shape[axis] for axis in AXES)

    def shards(trace_maps, sources, corner):
        maps = trace_maps[0, 0, 0]
        rows = sources[0, 0, 0]
        code = corner[0]
        if not fits_wave(sizes):
            return stepped(code, maps, rows)[None, None, None]
        lead = 1 - (jnp.right_shift(code, 1) & 1)
        code = jnp.where(lead == 1, 7 - code, code)
        kind = (code & 1) + 2 * (jnp.right_shift(code, 2) & 1)

        def branch(kind):
            return lambda *operands: wave(sizes, kind_bits(kind), *operands)

        traces = lax.switch(
            kind, [branch(kind) for kind in range(4)], lead.reshape(1), maps, rows
        )
        return traces[None, None, None]

    return jax.shard_map(
        shards,
        mesh=mesh,
        in_specs=(
            P("gx", "gy", "gz", None, None, None),
            P("gx", "gy", "gz", None, None, None),
            P(),
        ),
        out_specs=P("gx", "gy", "gz", None, None, None),
        check_vma=False,
    )
```

```python
import functools
import itertools

import jax
import jax.numpy as jnp
from jax import lax
from jax.experimental import pallas as pl
from jax.experimental.pallas import tpu as pltpu
from jax.sharding import PartitionSpec as P

STEPS = 6
AXES = ("gx", "gy", "gz")
ORDER = (0, 2, 1)
ROOM = pltpu.CompilerParams(vmem_limit_bytes=8 * 1024 * 1024)


def places(sizes):
    return itertools.product(*(range(size) for size in sizes))


def number(sizes, place):
    flat = 0
    for index, size in zip(place, sizes):
        flat = flat * size + index
    return flat


def depth_of(sizes, bits, place):
    return sum(
        index if bit else size - 1 - index for index, size, bit in zip(place, sizes, bits)
    )


def level_edges(sizes, bits, axis, level):
    edges = []
    for place in places(sizes):
        index = place[axis] + (1 if bits[axis] else -1)
        if 0 <= index < sizes[axis] and depth_of(sizes, bits, place) == level:
            edges.append((place, place[:axis] + (index,) + place[axis + 1 :]))
    return edges


def hop_edges(sizes, bits, axis, hop):
    back = tuple(1 - bit for bit in bits)
    return level_edges(sizes, bits, axis, hop - 1) + level_edges(sizes, back, axis, hop - 1)


def clash(edges):
    sources, targets = zip(*edges) if edges else ((), ())
    return len(set(sources)) < len(sources) or len(set(targets)) < len(targets)


def fits_wave(sizes):
    deepest = sum(size - 1 for size in sizes)
    return deepest <= STEPS + 1 and deepest % 2 == 1


SHARED = (
    (
        (0, 1, 2, -1, 3, 4, 5),
        (6, 7, 8, -2, 9, 10, 5),
        (6, 8, 7, -3, 10, 9, 5),
        (0, 11, 1, -3, 4, 3, 6),
    ),
    (
        (0, 1, 2, 3, 4, 5, 0),
        (6, 5, 7, 8, 1, 6, 3),
        (3, 6, 1, 0, 7, 5, 9),
        (1, 5, 10, 9, 2, 1, 0),
    ),
    (
        (0, 1, 2, -1, 3, 4, 5),
        (0, 6, 7, -2, 8, 9, 5),
        (6, 7, 10, -3, 9, 8, 11),
        (0, 2, 1, -4, 4, 11, 5),
    ),
)


def kind_bits(kind):
    return (kind & 1, 1, kind >> 1)


def swaps_of(sizes, axis, edges):
    twins = dict(edges)
    twins.update((target, source) for source, target in edges)
    for place in places(sizes):
        if place not in twins:
            line = [place[:axis] + (i,) + place[axis + 1 :] for i in range(sizes[axis])]
            left = [other for other in line if other not in twins and other != place]
            if left:
                twins[place], twins[left[0]] = left[0], place
    return set(twins.items())


def pairs_of(sizes, bits, axis, hop):
    deepest = sum(size - 1 for size in sizes)
    own = set(hop_edges(sizes, bits, axis, hop))
    number_of = SHARED[axis][bits[0] + 2 * bits[2]][hop - 1]
    edges = set(own)
    for kind, row in enumerate(SHARED[axis]):
        for other, found in enumerate(row, 1):
            if found == number_of and other <= deepest:
                edges.update(hop_edges(sizes, kind_bits(kind), axis, other))
    if number_of < 0:
        edges = swaps_of(sizes, axis, edges)
    if clash(sorted(edges)):
        edges = own
    assert not clash(sorted(edges)) and own <= edges
    return sorted((number(sizes, source), number(sizes, target)) for source, target in edges)


def my_depth(sizes, bits):
    return depth_of(sizes, bits, tuple(lax.axis_index(axis) for axis in AXES))


def chains_sent(hop, deepest):
    return range(max(0, hop - STEPS), min(max(0, deepest - STEPS), hop - 1) + 1)


def sooner(sizes, bits):
    return 2 * my_depth(sizes, bits) < sum(size - 1 for size in sizes)


def slots_by_arrival(sizes, bits, lead):
    first = jnp.where(sooner(sizes, bits), lead, 1 - lead)
    return first, 1 - first


def begin_kernel(sizes, bits, lead_hbm, sources_hbm, message_ref, lead_ref, raw_ref, arrived):
    deepest = sum(size - 1 for size in sizes)
    depth = my_depth(sizes, bits)

    @pl.when((depth == 0) | (depth == deepest))
    def _():
        copies = [
            pltpu.make_async_copy(sources_hbm, raw_ref, arrived.at[0]),
            pltpu.make_async_copy(lead_hbm, lead_ref, arrived.at[1]),
        ]
        for copy in copies:
            copy.start()
        for copy in copies:
            copy.wait()
        first, _ = slots_by_arrival(sizes, bits, lead_ref[0])
        message_ref[...] = raw_ref[first].astype(message_ref.dtype)


def begin(sizes, bits, lead, sources):
    hbm = pl.BlockSpec(memory_space=pl.ANY)
    return pl.pallas_call(
        functools.partial(begin_kernel, sizes, bits),
        out_shape=pltpu.VMEM(sources.shape[1:], jnp.bfloat16),
        in_specs=[hbm, hbm],
        out_specs=pl.BlockSpec(memory_space=pltpu.VMEM),
        scratch_shapes=[
            pltpu.SMEM(lead.shape, lead.dtype),
            pltpu.VMEM(sources.shape, sources.dtype),
            pltpu.SemaphoreType.DMA((2,)),
        ],
        compiler_params=ROOM,
        name="begin",
    )(lead, sources)


def load_first_kernel(
    sizes, bits, lead_ref, maps_hbm, sources_hbm, after_ref, map_ref, held_ref, traces_ref, arrived
):
    slots = slots_by_arrival(sizes, bits, lead_ref[0])
    copies = [
        pltpu.make_async_copy(sources_hbm.at[slot], held_ref.at[place], arrived.at[place])
        for place, slot in enumerate(slots)
    ]
    copies.append(pltpu.make_async_copy(maps_hbm.at[slots[0]], map_ref, arrived.at[2]))
    for copy in copies:
        copy.start()
    for copy in copies:
        copy.wait()
    traces_ref[...] = held_ref[...].astype(traces_ref.dtype)


def load_first(sizes, bits, lead, maps, sources, after):
    hbm = pl.BlockSpec(memory_space=pl.ANY)
    vmem = pl.BlockSpec(memory_space=pltpu.VMEM)
    return pl.pallas_call(
        functools.partial(load_first_kernel, sizes, bits),
        out_shape=(
            pltpu.VMEM(maps.shape[1:], maps.dtype),
            pltpu.VMEM(sources.shape, sources.dtype),
            pltpu.VMEM(sources.shape, jnp.bfloat16),
        ),
        in_specs=[pl.BlockSpec(memory_space=pltpu.SMEM), hbm, hbm, vmem],
        out_specs=(vmem, vmem, vmem),
        scratch_shapes=[pltpu.SemaphoreType.DMA((3,))],
        compiler_params=ROOM,
        name="load_first",
    )(lead, maps, sources, pltpu.with_memory_space_constraint(after, pltpu.VMEM))


def load_second_kernel(sizes, bits, lead_ref, maps_hbm, after_ref, map_ref, arrived):
    _, slot = slots_by_arrival(sizes, bits, lead_ref[0])
    copy = pltpu.make_async_copy(maps_hbm.at[slot], map_ref, arrived)
    copy.start()
    copy.wait()


def load_second(sizes, bits, lead, maps, after):
    hbm = pl.BlockSpec(memory_space=pl.ANY)
    vmem = pl.BlockSpec(memory_space=pltpu.VMEM)
    return pl.pallas_call(
        functools.partial(load_second_kernel, sizes, bits),
        out_shape=pltpu.VMEM(maps.shape[1:], maps.dtype),
        in_specs=[pl.BlockSpec(memory_space=pltpu.SMEM), hbm, vmem],
        out_specs=vmem,
        scratch_shapes=[pltpu.SemaphoreType.DMA(())],
        compiler_params=ROOM,
        name="load_second",
    )(lead, maps, pltpu.with_memory_space_constraint(after, pltpu.VMEM))


def chains_sent(hop, deepest):
    return range(max(0, hop - STEPS), min(max(0, deepest - STEPS), hop - 1) + 1)


def hop_kernel(
    hop, sizes, bits, lead_ref, y_ref, z_ref, x_ref, sources_ref, old_ref, *refs
):
    deepest = sum(size - 1 for size in sizes)
    depth = my_depth(sizes, bits)
    last = hop == deepest
    results = refs[-1:] if last else refs[-2:]
    map_ref = refs[0]
    traces_ref = results[-1]
    rows = sources_ref.shape[1]
    turn = 0 if 2 * hop < deepest else 1

    def place_of(turn):
        return slots_by_arrival(sizes, bits, lead_ref[0])[turn] if last else turn

    for kept in range(2):
        traces_ref[place_of(kept)] = old_ref[kept]

    @pl.when((depth == hop) | (depth == deepest - hop))
    def _():
        summed = None
        for axis, ref in enumerate((x_ref, y_ref, z_ref)):
            index = lax.axis_index(AXES[axis])
            lower, upper = index > 0, index < sizes[axis] - 1
            inside = jnp.where(
                (depth == hop) == bool(bits[axis]), lower.astype(jnp.int32), upper.astype(jnp.int32)
            )
            came = jnp.where(inside == 1, ref[...].astype(jnp.float32), 0.0)
            summed = came if summed is None else summed + came
        mapped = jnp.dot(
            summed.astype(jnp.bfloat16), map_ref[...], preferred_element_type=jnp.float32
        )
        source = sources_ref[turn]
        came = chains_sent(hop, deepest)
        kept = came if last else chains_sent(hop + 1, deepest)
        for chain in sorted({*came, *kept}):
            if chain in came:
                at = came.index(chain) * rows
                new = (mapped[at : at + rows] + source).astype(jnp.bfloat16)
            else:
                new = source.astype(jnp.bfloat16)
            if not last and chain in kept:
                at = kept.index(chain) * rows
                results[0][at : at + rows] = new
            if chain == max(0, hop - STEPS):
                traces_ref[place_of(turn)] = new


def take_hop(hop, sizes, bits, lead, came, maps, sources, traces):
    deepest = sum(size - 1 for size in sizes)
    last = hop == deepest
    vmem = pl.BlockSpec(memory_space=pltpu.VMEM)
    held = [came[axis] for axis in reversed(ORDER)] + [sources, traces] + maps
    held = [pltpu.with_memory_space_constraint(a, pltpu.VMEM) for a in held]
    shapes = (jax.ShapeDtypeStruct(traces.shape, traces.dtype),)
    if not last:
        message = (len(chains_sent(hop + 1, deepest)) * sources.shape[1], sources.shape[2])
        shapes = (
            pltpu.VMEM(message, traces.dtype),
            pltpu.VMEM(traces.shape, traces.dtype),
        )
    results = pl.pallas_call(
        functools.partial(hop_kernel, hop, sizes, bits),
        out_shape=shapes,
        in_specs=[pl.BlockSpec(memory_space=pltpu.SMEM if last else pl.ANY)] + [vmem] * len(held),
        out_specs=(vmem,) * len(shapes),
        compiler_params=ROOM,
        name=f"hop{hop}",
    )(lead, *held)
    return results[0], results[-1]


def wave(sizes, bits, lead, maps, sources):
    deepest = sum(size - 1 for size in sizes)
    message = begin(sizes, bits, lead, sources)
    later = min(2, deepest)
    for hop in range(1, deepest + 1):
        came = [None] * 3
        for axis in ORDER:
            came[axis] = lax.ppermute(message, AXES, pairs_of(sizes, bits, axis, hop))
        if hop == 1:
            first, sources, traces = load_first(sizes, bits, lead, maps, sources, message)
        if hop == later:
            second = load_second(sizes, bits, lead, maps, message)
        used = [first] if 2 * hop < deepest else [second]
        if hop == later and 2 * hop < deepest:
            used.append(second)
        message, traces = take_hop(hop, sizes, bits, lead, came, used, sources, traces)
    return traces


def passed_along(array, axis, by):
    devices = lax.axis_size(axis)
    pairs = [(i, i + by) for i in range(devices) if 0 <= i + by < devices]
    return lax.ppermute(array, axis, pairs)


def stepped(code, maps, sources):
    traces = sources.astype(jnp.bfloat16)
    for _ in range(STEPS):
        incoming = jnp.zeros(sources.shape, jnp.float32)
        for position, axis in enumerate(AXES):
            up = (jnp.right_shift(code, position) & 1) == 1
            lower = passed_along(jnp.where(up, traces[0], traces[1]), axis, 1)
            upper = passed_along(jnp.where(up, traces[1], traces[0]), axis, -1)
            came = jnp.stack([jnp.where(up, lower, upper), jnp.where(up, upper, lower)])
            incoming = incoming + came.astype(jnp.float32)
        mapped = jnp.einsum(
            "scf,sfg->scg", incoming.astype(jnp.bfloat16), maps, preferred_element_type=jnp.float32
        )
        traces = (mapped + sources).astype(jnp.bfloat16)
    return traces


def solution(mesh):
    sizes = tuple(mesh.shape[axis] for axis in AXES)

    def shards(trace_maps, sources, corner):
        maps = trace_maps[0, 0, 0]
        rows = sources[0, 0, 0]
        code = corner[0]
        if not fits_wave(sizes):
            return stepped(code, maps, rows)[None, None, None]
        lead = 1 - (jnp.right_shift(code, 1) & 1)
        code = jnp.where(lead == 1, 7 - code, code)
        kind = (code & 1) + 2 * (jnp.right_shift(code, 2) & 1)

        def branch(kind):
            return lambda *operands: wave(sizes, kind_bits(kind), *operands)

        traces = lax.switch(
            kind, [branch(kind) for kind in range(4)], lead.reshape(1), maps, rows
        )
        return traces[None, None, None]

    return jax.shard_map(
        shards,
        mesh=mesh,
        in_specs=(
            P("gx", "gy", "gz", None, None, None),
            P("gx", "gy", "gz", None, None, None),
            P(),
        ),
        out_specs=P("gx", "gy", "gz", None, None, None),
        check_vma=False,
    )
```

```python
import functools
import itertools

import jax
import jax.numpy as jnp
from jax import lax
from jax.experimental import pallas as pl
from jax.experimental.pallas import tpu as pltpu
from jax.sharding import PartitionSpec as P

STEPS = 6
AXES = ("gx", "gy", "gz")
ORDER = (0, 2, 1)
ROOM = pltpu.CompilerParams(vmem_limit_bytes=8 * 1024 * 1024)


def places(sizes):
    return itertools.product(*(range(size) for size in sizes))


def number(sizes, place):
    flat = 0
    for index, size in zip(place, sizes):
        flat = flat * size + index
    return flat


def depth_of(sizes, bits, place):
    return sum(
        index if bit else size - 1 - index for index, size, bit in zip(place, sizes, bits)
    )


def level_edges(sizes, bits, axis, level):
    edges = []
    for place in places(sizes):
        index = place[axis] + (1 if bits[axis] else -1)
        if 0 <= index < sizes[axis] and depth_of(sizes, bits, place) == level:
            edges.append((place, place[:axis] + (index,) + place[axis + 1 :]))
    return edges


def hop_edges(sizes, bits, axis, hop):
    back = tuple(1 - bit for bit in bits)
    return level_edges(sizes, bits, axis, hop - 1) + level_edges(sizes, back, axis, hop - 1)


def clash(edges):
    sources, targets = zip(*edges) if edges else ((), ())
    return len(set(sources)) < len(sources) or len(set(targets)) < len(targets)


def fits_wave(sizes):
    deepest = sum(size - 1 for size in sizes)
    return deepest <= STEPS + 1 and deepest % 2 == 1


SHARED = (
    (
        (0, 1, 2, -1, 3, 4, 3),
        (5, 6, 7, -2, 8, 9, 8),
        (5, 7, 6, -3, 9, 8, 9),
        (0, 2, 1, -4, 4, 3, 4),
    ),
    (
        (0, 1, 2, -1, 3, 4, 5),
        (4, 6, 7, -2, 8, 0, 5),
        (5, 0, 9, -3, 10, 6, 0),
        (6, 4, 11, -3, 2, 12, 4),
    ),
    (
        (0, 1, 2, -1, 3, 4, 3),
        (5, 6, 7, -2, 8, 9, 8),
        (6, 5, 10, -3, 9, 8, 9),
        (1, 0, 11, -2, 4, 3, 4),
    ),
)


def kind_bits(kind):
    return (kind & 1, 1, kind >> 1)


def swaps_of(sizes, axis, edges):
    twins = dict(edges)
    twins.update((target, source) for source, target in edges)
    for place in places(sizes):
        if place not in twins:
            line = [place[:axis] + (i,) + place[axis + 1 :] for i in range(sizes[axis])]
            left = [other for other in line if other not in twins and other != place]
            if left:
                twins[place], twins[left[0]] = left[0], place
    return set(twins.items())


def pairs_of(sizes, bits, axis, hop):
    deepest = sum(size - 1 for size in sizes)
    own = set(hop_edges(sizes, bits, axis, hop))
    number_of = SHARED[axis][bits[0] + 2 * bits[2]][hop - 1]
    edges = set(own)
    for kind, row in enumerate(SHARED[axis]):
        for other, found in enumerate(row, 1):
            if found == number_of and other <= deepest:
                edges.update(hop_edges(sizes, kind_bits(kind), axis, other))
    if number_of < 0:
        edges = swaps_of(sizes, axis, edges)
    if clash(sorted(edges)):
        edges = own
    assert not clash(sorted(edges)) and own <= edges
    return sorted((number(sizes, source), number(sizes, target)) for source, target in edges)


def my_depth(sizes, bits):
    return depth_of(sizes, bits, tuple(lax.axis_index(axis) for axis in AXES))


def chains_sent(hop, deepest):
    return range(max(0, hop - STEPS), min(max(0, deepest - STEPS), hop - 1) + 1)


def sooner(sizes, bits):
    return 2 * my_depth(sizes, bits) < sum(size - 1 for size in sizes)


def slots_by_arrival(sizes, bits, lead):
    first = jnp.where(sooner(sizes, bits), lead, 1 - lead)
    return first, 1 - first


def begin_kernel(sizes, bits, lead_hbm, sources_hbm, message_ref, lead_ref, raw_ref, arrived):
    deepest = sum(size - 1 for size in sizes)
    depth = my_depth(sizes, bits)

    @pl.when((depth == 0) | (depth == deepest))
    def _():
        copies = [
            pltpu.make_async_copy(sources_hbm, raw_ref, arrived.at[0]),
            pltpu.make_async_copy(lead_hbm, lead_ref, arrived.at[1]),
        ]
        for copy in copies:
            copy.start()
        for copy in copies:
            copy.wait()
        first, _ = slots_by_arrival(sizes, bits, lead_ref[0])
        message_ref[...] = raw_ref[first].astype(message_ref.dtype)


def begin(sizes, bits, lead, sources):
    hbm = pl.BlockSpec(memory_space=pl.ANY)
    return pl.pallas_call(
        functools.partial(begin_kernel, sizes, bits),
        out_shape=pltpu.VMEM(sources.shape[1:], jnp.bfloat16),
        in_specs=[hbm, hbm],
        out_specs=pl.BlockSpec(memory_space=pltpu.VMEM),
        scratch_shapes=[
            pltpu.SMEM(lead.shape, lead.dtype),
            pltpu.VMEM(sources.shape, sources.dtype),
            pltpu.SemaphoreType.DMA((2,)),
        ],
        compiler_params=ROOM,
        name="begin",
    )(lead, sources)


def load_first_kernel(
    sizes, bits, lead_ref, maps_hbm, sources_hbm, after_ref, map_ref, held_ref, traces_ref, arrived
):
    slots = slots_by_arrival(sizes, bits, lead_ref[0])
    copies = [
        pltpu.make_async_copy(sources_hbm.at[slot], held_ref.at[place], arrived.at[place])
        for place, slot in enumerate(slots)
    ]
    copies.append(pltpu.make_async_copy(maps_hbm.at[slots[0]], map_ref, arrived.at[2]))
    for copy in copies:
        copy.start()
    for copy in copies:
        copy.wait()
    traces_ref[...] = held_ref[...].astype(traces_ref.dtype)


def load_first(sizes, bits, lead, maps, sources, after):
    hbm = pl.BlockSpec(memory_space=pl.ANY)
    vmem = pl.BlockSpec(memory_space=pltpu.VMEM)
    return pl.pallas_call(
        functools.partial(load_first_kernel, sizes, bits),
        out_shape=(
            pltpu.VMEM(maps.shape[1:], maps.dtype),
            pltpu.VMEM(sources.shape, sources.dtype),
            pltpu.VMEM(sources.shape, jnp.bfloat16),
        ),
        in_specs=[pl.BlockSpec(memory_space=pltpu.SMEM), hbm, hbm, vmem],
        out_specs=(vmem, vmem, vmem),
        scratch_shapes=[pltpu.SemaphoreType.DMA((3,))],
        compiler_params=ROOM,
        name="load_first",
    )(lead, maps, sources, pltpu.with_memory_space_constraint(after, pltpu.VMEM))


def load_second_kernel(sizes, bits, lead_ref, maps_hbm, after_ref, map_ref, arrived):
    _, slot = slots_by_arrival(sizes, bits, lead_ref[0])
    copy = pltpu.make_async_copy(maps_hbm.at[slot], map_ref, arrived)
    copy.start()
    copy.wait()


def load_second(sizes, bits, lead, maps, after):
    hbm = pl.BlockSpec(memory_space=pl.ANY)
    vmem = pl.BlockSpec(memory_space=pltpu.VMEM)
    return pl.pallas_call(
        functools.partial(load_second_kernel, sizes, bits),
        out_shape=pltpu.VMEM(maps.shape[1:], maps.dtype),
        in_specs=[pl.BlockSpec(memory_space=pltpu.SMEM), hbm, vmem],
        out_specs=vmem,
        scratch_shapes=[pltpu.SemaphoreType.DMA(())],
        compiler_params=ROOM,
        name="load_second",
    )(lead, maps, pltpu.with_memory_space_constraint(after, pltpu.VMEM))


def chains_sent(hop, deepest):
    return range(max(0, hop - STEPS), min(max(0, deepest - STEPS), hop - 1) + 1)


def hop_kernel(
    hop, sizes, bits, lead_ref, y_ref, z_ref, x_ref, sources_ref, old_ref, *refs
):
    deepest = sum(size - 1 for size in sizes)
    depth = my_depth(sizes, bits)
    last = hop == deepest
    results = refs[-1:] if last else refs[-2:]
    map_ref = refs[0]
    traces_ref = results[-1]
    rows = sources_ref.shape[1]
    turn = 0 if 2 * hop < deepest else 1

    def place_of(turn):
        return slots_by_arrival(sizes, bits, lead_ref[0])[turn] if last else turn

    for kept in range(2):
        traces_ref[place_of(kept)] = old_ref[kept]

    @pl.when((depth == hop) | (depth == deepest - hop))
    def _():
        summed = None
        for axis, ref in enumerate((x_ref, y_ref, z_ref)):
            index = lax.axis_index(AXES[axis])
            lower, upper = index > 0, index < sizes[axis] - 1
            inside = jnp.where(
                (depth == hop) == bool(bits[axis]), lower.astype(jnp.int32), upper.astype(jnp.int32)
            )
            came = jnp.where(inside == 1, ref[...].astype(jnp.float32), 0.0)
            summed = came if summed is None else summed + came
        mapped = jnp.dot(
            summed.astype(jnp.bfloat16), map_ref[...], preferred_element_type=jnp.float32
        )
        source = sources_ref[turn]
        came = chains_sent(hop, deepest)
        kept = came if last else chains_sent(hop + 1, deepest)
        for chain in sorted({*came, *kept}):
            if chain in came:
                at = came.index(chain) * rows
                new = (mapped[at : at + rows] + source).astype(jnp.bfloat16)
            else:
                new = source.astype(jnp.bfloat16)
            if not last and chain in kept:
                at = kept.index(chain) * rows
                results[0][at : at + rows] = new
            if chain == max(0, hop - STEPS):
                traces_ref[place_of(turn)] = new


def take_hop(hop, sizes, bits, lead, came, maps, sources, traces):
    deepest = sum(size - 1 for size in sizes)
    last = hop == deepest
    vmem = pl.BlockSpec(memory_space=pltpu.VMEM)
    held = [came[axis] for axis in reversed(ORDER)] + [sources, traces] + maps
    held = [pltpu.with_memory_space_constraint(a, pltpu.VMEM) for a in held]
    shapes = (jax.ShapeDtypeStruct(traces.shape, traces.dtype),)
    if not last:
        message = (len(chains_sent(hop + 1, deepest)) * sources.shape[1], sources.shape[2])
        shapes = (
            pltpu.VMEM(message, traces.dtype),
            pltpu.VMEM(traces.shape, traces.dtype),
        )
    results = pl.pallas_call(
        functools.partial(hop_kernel, hop, sizes, bits),
        out_shape=shapes,
        in_specs=[pl.BlockSpec(memory_space=pltpu.SMEM if last else pl.ANY)] + [vmem] * len(held),
        out_specs=(vmem,) * len(shapes),
        compiler_params=ROOM,
        name=f"hop{hop}",
    )(lead, *held)
    return results[0], results[-1]


def wave(sizes, bits, lead, maps, sources):
    deepest = sum(size - 1 for size in sizes)
    message = begin(sizes, bits, lead, sources)
    later = min(2, deepest)
    for hop in range(1, deepest + 1):
        came = [None] * 3
        for axis in ORDER:
            came[axis] = lax.ppermute(message, AXES, pairs_of(sizes, bits, axis, hop))
        if hop == 1:
            first, sources, traces = load_first(sizes, bits, lead, maps, sources, message)
        if hop == later:
            second = load_second(sizes, bits, lead, maps, message)
        used = [first] if 2 * hop < deepest else [second]
        if hop == later and 2 * hop < deepest:
            used.append(second)
        message, traces = take_hop(hop, sizes, bits, lead, came, used, sources, traces)
    return traces


def passed_along(array, axis, by):
    devices = lax.axis_size(axis)
    pairs = [(i, i + by) for i in range(devices) if 0 <= i + by < devices]
    return lax.ppermute(array, axis, pairs)


def stepped(code, maps, sources):
    traces = sources.astype(jnp.bfloat16)
    for _ in range(STEPS):
        incoming = jnp.zeros(sources.shape, jnp.float32)
        for position, axis in enumerate(AXES):
            up = (jnp.right_shift(code, position) & 1) == 1
            lower = passed_along(jnp.where(up, traces[0], traces[1]), axis, 1)
            upper = passed_along(jnp.where(up, traces[1], traces[0]), axis, -1)
            came = jnp.stack([jnp.where(up, lower, upper), jnp.where(up, upper, lower)])
            incoming = incoming + came.astype(jnp.float32)
        mapped = jnp.einsum(
            "scf,sfg->scg", incoming.astype(jnp.bfloat16), maps, preferred_element_type=jnp.float32
        )
        traces = (mapped + sources).astype(jnp.bfloat16)
    return traces


def solution(mesh):
    sizes = tuple(mesh.shape[axis] for axis in AXES)

    def shards(trace_maps, sources, corner):
        maps = trace_maps[0, 0, 0]
        rows = sources[0, 0, 0]
        code = corner[0]
        if not fits_wave(sizes):
            return stepped(code, maps, rows)[None, None, None]
        lead = 1 - (jnp.right_shift(code, 1) & 1)
        code = jnp.where(lead == 1, 7 - code, code)
        kind = (code & 1) + 2 * (jnp.right_shift(code, 2) & 1)

        def branch(kind):
            return lambda *operands: wave(sizes, kind_bits(kind), *operands)

        traces = lax.switch(
            kind, [branch(kind) for kind in range(4)], lead.reshape(1), maps, rows
        )
        return traces[None, None, None]

    return jax.shard_map(
        shards,
        mesh=mesh,
        in_specs=(
            P("gx", "gy", "gz", None, None, None),
            P("gx", "gy", "gz", None, None, None),
            P(),
        ),
        out_specs=P("gx", "gy", "gz", None, None, None),
        check_vma=False,
    )
```

```python
import functools
import itertools

import jax
import jax.numpy as jnp
from jax import lax
from jax.experimental import pallas as pl
from jax.experimental.pallas import tpu as pltpu
from jax.sharding import PartitionSpec as P

STEPS = 6
AXES = ("gx", "gy", "gz")
ORDER = (0, 2, 1)
ROOM = pltpu.CompilerParams(vmem_limit_bytes=8 * 1024 * 1024)


def places(sizes):
    return itertools.product(*(range(size) for size in sizes))


def number(sizes, place):
    flat = 0
    for index, size in zip(place, sizes):
        flat = flat * size + index
    return flat


def depth_of(sizes, bits, place):
    return sum(
        index if bit else size - 1 - index for index, size, bit in zip(place, sizes, bits)
    )


def level_edges(sizes, bits, axis, level):
    edges = []
    for place in places(sizes):
        index = place[axis] + (1 if bits[axis] else -1)
        if 0 <= index < sizes[axis] and depth_of(sizes, bits, place) == level:
            edges.append((place, place[:axis] + (index,) + place[axis + 1 :]))
    return edges


def hop_edges(sizes, bits, axis, hop):
    back = tuple(1 - bit for bit in bits)
    return level_edges(sizes, bits, axis, hop - 1) + level_edges(sizes, back, axis, hop - 1)


def clash(edges):
    sources, targets = zip(*edges) if edges else ((), ())
    return len(set(sources)) < len(sources) or len(set(targets)) < len(targets)


def fits_wave(sizes):
    deepest = sum(size - 1 for size in sizes)
    return deepest <= STEPS + 1 and deepest % 2 == 1


SHARED = (
    (
        (0, 1, 2, -1, 3, 4, 3),
        (5, 6, 7, -2, 8, 9, 8),
        (5, 7, 6, -3, 9, 8, 9),
        (0, 2, 1, -4, 4, 3, 4),
    ),
    (
        (0, 1, 2, -1, 3, 4, 5),
        (4, 6, 7, -2, 8, 0, 5),
        (5, 0, 9, -3, 10, 6, 0),
        (6, 4, 11, -3, 2, 12, 4),
    ),
    (
        (0, 1, 2, -1, 3, 4, 3),
        (5, 6, 7, -2, 8, 9, 8),
        (6, 5, 10, -3, 9, 8, 9),
        (1, 0, 11, -2, 4, 3, 4),
    ),
)


def kind_bits(kind):
    return (kind & 1, 1, kind >> 1)


def swaps_of(sizes, axis, edges):
    twins = dict(edges)
    twins.update((target, source) for source, target in edges)
    for place in places(sizes):
        if place not in twins:
            line = [place[:axis] + (i,) + place[axis + 1 :] for i in range(sizes[axis])]
            left = [other for other in line if other not in twins and other != place]
            if left:
                twins[place], twins[left[0]] = left[0], place
    return set(twins.items())


def pairs_of(sizes, bits, axis, hop):
    deepest = sum(size - 1 for size in sizes)
    own = set(hop_edges(sizes, bits, axis, hop))
    number_of = SHARED[axis][bits[0] + 2 * bits[2]][hop - 1]
    edges = set(own)
    for kind, row in enumerate(SHARED[axis]):
        for other, found in enumerate(row, 1):
            if found == number_of and other <= deepest:
                edges.update(hop_edges(sizes, kind_bits(kind), axis, other))
    if number_of < 0:
        edges = swaps_of(sizes, axis, edges)
    if clash(sorted(edges)):
        edges = own
    assert not clash(sorted(edges)) and own <= edges
    return sorted((number(sizes, source), number(sizes, target)) for source, target in edges)


def my_depth(sizes, bits):
    return depth_of(sizes, bits, tuple(lax.axis_index(axis) for axis in AXES))


def chains_sent(hop, deepest):
    return range(max(0, hop - STEPS), min(max(0, deepest - STEPS), hop - 1) + 1)


def sooner(sizes, bits):
    return 2 * my_depth(sizes, bits) < sum(size - 1 for size in sizes)


def slots_by_arrival(sizes, bits, lead):
    first = jnp.where(sooner(sizes, bits), lead, 1 - lead)
    return first, 1 - first


def begin_kernel(sizes, bits, lead_hbm, sources_hbm, message_ref, lead_ref, raw_ref, arrived):
    deepest = sum(size - 1 for size in sizes)
    depth = my_depth(sizes, bits)

    @pl.when((depth == 0) | (depth == deepest))
    def _():
        copies = [
            pltpu.make_async_copy(sources_hbm, raw_ref, arrived.at[0]),
            pltpu.make_async_copy(lead_hbm, lead_ref, arrived.at[1]),
        ]
        for copy in copies:
            copy.start()
        for copy in copies:
            copy.wait()
        first, _ = slots_by_arrival(sizes, bits, lead_ref[0])
        message_ref[...] = raw_ref[first].astype(message_ref.dtype)


def begin(sizes, bits, lead, sources):
    hbm = pl.BlockSpec(memory_space=pl.ANY)
    return pl.pallas_call(
        functools.partial(begin_kernel, sizes, bits),
        out_shape=pltpu.VMEM(sources.shape[1:], jnp.bfloat16),
        in_specs=[hbm, hbm],
        out_specs=pl.BlockSpec(memory_space=pltpu.VMEM),
        scratch_shapes=[
            pltpu.SMEM(lead.shape, lead.dtype),
            pltpu.VMEM(sources.shape, sources.dtype),
            pltpu.SemaphoreType.DMA((2,)),
        ],
        compiler_params=ROOM,
        name="begin",
    )(lead, sources)


def load_first_kernel(
    sizes, bits, lead_ref, maps_hbm, sources_hbm, after_ref, map_ref, held_ref, traces_ref, arrived
):
    slots = slots_by_arrival(sizes, bits, lead_ref[0])
    copies = [
        pltpu.make_async_copy(sources_hbm.at[slot], held_ref.at[place], arrived.at[place])
        for place, slot in enumerate(slots)
    ]
    copies.append(pltpu.make_async_copy(maps_hbm.at[slots[0]], map_ref, arrived.at[2]))
    for copy in copies:
        copy.start()
    for copy in copies:
        copy.wait()
    traces_ref[...] = held_ref[...].astype(traces_ref.dtype)


def load_first(sizes, bits, lead, maps, sources, after):
    hbm = pl.BlockSpec(memory_space=pl.ANY)
    vmem = pl.BlockSpec(memory_space=pltpu.VMEM)
    return pl.pallas_call(
        functools.partial(load_first_kernel, sizes, bits),
        out_shape=(
            pltpu.VMEM(maps.shape[1:], maps.dtype),
            pltpu.VMEM(sources.shape, sources.dtype),
            pltpu.VMEM(sources.shape, jnp.bfloat16),
        ),
        in_specs=[pl.BlockSpec(memory_space=pltpu.SMEM), hbm, hbm, vmem],
        out_specs=(vmem, vmem, vmem),
        scratch_shapes=[pltpu.SemaphoreType.DMA((3,))],
        compiler_params=ROOM,
        name="load_first",
    )(lead, maps, sources, pltpu.with_memory_space_constraint(after, pltpu.VMEM))


def load_second_kernel(sizes, bits, lead_ref, maps_hbm, after_ref, map_ref, arrived):
    _, slot = slots_by_arrival(sizes, bits, lead_ref[0])
    copy = pltpu.make_async_copy(maps_hbm.at[slot], map_ref, arrived)
    copy.start()
    copy.wait()


def load_second(sizes, bits, lead, maps, after):
    hbm = pl.BlockSpec(memory_space=pl.ANY)
    vmem = pl.BlockSpec(memory_space=pltpu.VMEM)
    return pl.pallas_call(
        functools.partial(load_second_kernel, sizes, bits),
        out_shape=pltpu.VMEM(maps.shape[1:], maps.dtype),
        in_specs=[pl.BlockSpec(memory_space=pltpu.SMEM), hbm, vmem],
        out_specs=vmem,
        scratch_shapes=[pltpu.SemaphoreType.DMA(())],
        compiler_params=ROOM,
        name="load_second",
    )(lead, maps, pltpu.with_memory_space_constraint(after, pltpu.VMEM))


def chains_sent(hop, deepest):
    return range(max(0, hop - STEPS), min(max(0, deepest - STEPS), hop - 1) + 1)


def hop_kernel(
    hop, sizes, bits, lead_ref, y_ref, z_ref, x_ref, sources_ref, old_ref, *refs
):
    deepest = sum(size - 1 for size in sizes)
    depth = my_depth(sizes, bits)
    last = hop == deepest
    if last:
        *refs, out_ref, kept_ref, sent = refs
        slots = slots_by_arrival(sizes, bits, lead_ref[0])
        early = pltpu.make_async_copy(old_ref.at[0], out_ref.at[slots[0]], sent.at[0])
        early.start()
        refs = [*refs, kept_ref]
    results = refs[-1:] if last else refs[-2:]
    map_ref = refs[0]
    traces_ref = results[-1]
    rows = sources_ref.shape[1]
    turn = 0 if 2 * hop < deepest else 1
    assert turn == 1 or not last

    for kept in range(2):
        traces_ref[kept] = old_ref[kept]

    @pl.when((depth == hop) | (depth == deepest - hop))
    def _():
        summed = None
        for axis, ref in enumerate((x_ref, y_ref, z_ref)):
            index = lax.axis_index(AXES[axis])
            lower, upper = index > 0, index < sizes[axis] - 1
            inside = jnp.where(
                (depth == hop) == bool(bits[axis]), lower.astype(jnp.int32), upper.astype(jnp.int32)
            )
            came = jnp.where(inside == 1, ref[...].astype(jnp.float32), 0.0)
            summed = came if summed is None else summed + came
        mapped = jnp.dot(
            summed.astype(jnp.bfloat16), map_ref[...], preferred_element_type=jnp.float32
        )
        source = sources_ref[turn]
        came = chains_sent(hop, deepest)
        kept = came if last else chains_sent(hop + 1, deepest)
        for chain in sorted({*came, *kept}):
            if chain in came:
                at = came.index(chain) * rows
                new = (mapped[at : at + rows] + source).astype(jnp.bfloat16)
            else:
                new = source.astype(jnp.bfloat16)
            if not last and chain in kept:
                at = kept.index(chain) * rows
                results[0][at : at + rows] = new
            if chain == max(0, hop - STEPS):
                traces_ref[turn] = new

    if last:
        late = pltpu.make_async_copy(kept_ref.at[1], out_ref.at[slots[1]], sent.at[1])
        late.start()
        early.wait()
        late.wait()


def take_hop(hop, sizes, bits, lead, came, maps, sources, traces):
    deepest = sum(size - 1 for size in sizes)
    last = hop == deepest
    vmem = pl.BlockSpec(memory_space=pltpu.VMEM)
    held = [came[axis] for axis in reversed(ORDER)] + [sources, traces] + maps
    held = [pltpu.with_memory_space_constraint(a, pltpu.VMEM) for a in held]
    shapes = (pltpu.HBM(traces.shape, traces.dtype),)
    if not last:
        message = (len(chains_sent(hop + 1, deepest)) * sources.shape[1], sources.shape[2])
        shapes = (
            pltpu.VMEM(message, traces.dtype),
            pltpu.VMEM(traces.shape, traces.dtype),
        )
    results = pl.pallas_call(
        functools.partial(hop_kernel, hop, sizes, bits),
        out_shape=shapes,
        in_specs=[pl.BlockSpec(memory_space=pltpu.SMEM if last else pl.ANY)] + [vmem] * len(held),
        out_specs=(pl.BlockSpec(memory_space=pl.ANY),) if last else (vmem,) * len(shapes),
        scratch_shapes=[
            pltpu.VMEM(traces.shape, traces.dtype),
            pltpu.SemaphoreType.DMA((2,)),
        ] if last else [],
        compiler_params=ROOM,
        name=f"hop{hop}",
    )(lead, *held)
    return results[0], results[-1]


def wave(sizes, bits, lead, maps, sources):
    deepest = sum(size - 1 for size in sizes)
    message = begin(sizes, bits, lead, sources)
    later = min(2, deepest)
    for hop in range(1, deepest + 1):
        came = [None] * 3
        for axis in ORDER:
            came[axis] = lax.ppermute(message, AXES, pairs_of(sizes, bits, axis, hop))
        if hop == 1:
            first, sources, traces = load_first(sizes, bits, lead, maps, sources, message)
        if hop == later:
            second = load_second(sizes, bits, lead, maps, message)
        used = [first] if 2 * hop < deepest else [second]
        if hop == later and 2 * hop < deepest:
            used.append(second)
        message, traces = take_hop(hop, sizes, bits, lead, came, used, sources, traces)
    return traces


def passed_along(array, axis, by):
    devices = lax.axis_size(axis)
    pairs = [(i, i + by) for i in range(devices) if 0 <= i + by < devices]
    return lax.ppermute(array, axis, pairs)


def stepped(code, maps, sources):
    traces = sources.astype(jnp.bfloat16)
    for _ in range(STEPS):
        incoming = jnp.zeros(sources.shape, jnp.float32)
        for position, axis in enumerate(AXES):
            up = (jnp.right_shift(code, position) & 1) == 1
            lower = passed_along(jnp.where(up, traces[0], traces[1]), axis, 1)
            upper = passed_along(jnp.where(up, traces[1], traces[0]), axis, -1)
            came = jnp.stack([jnp.where(up, lower, upper), jnp.where(up, upper, lower)])
            incoming = incoming + came.astype(jnp.float32)
        mapped = jnp.einsum(
            "scf,sfg->scg", incoming.astype(jnp.bfloat16), maps, preferred_element_type=jnp.float32
        )
        traces = (mapped + sources).astype(jnp.bfloat16)
    return traces


def solution(mesh):
    sizes = tuple(mesh.shape[axis] for axis in AXES)

    def shards(trace_maps, sources, corner):
        maps = trace_maps[0, 0, 0]
        rows = sources[0, 0, 0]
        code = corner[0]
        if not fits_wave(sizes):
            return stepped(code, maps, rows)[None, None, None]
        lead = 1 - (jnp.right_shift(code, 1) & 1)
        code = jnp.where(lead == 1, 7 - code, code)
        kind = (code & 1) + 2 * (jnp.right_shift(code, 2) & 1)

        def branch(kind):
            return lambda *operands: wave(sizes, kind_bits(kind), *operands)

        traces = lax.switch(
            kind, [branch(kind) for kind in range(4)], lead.reshape(1), maps, rows
        )
        return traces[None, None, None]

    return jax.shard_map(
        shards,
        mesh=mesh,
        in_specs=(
            P("gx", "gy", "gz", None, None, None),
            P("gx", "gy", "gz", None, None, None),
            P(),
        ),
        out_specs=P("gx", "gy", "gz", None, None, None),
        check_vma=False,
    )
```
